128 devices in a mesh: tok: 8 (over x, core), head: 8 (over y, z_hi), seq: 2 (over z_lo).
Axes of the slice: x: 4, y: 4, z: 4 (z_hi: 2, z_lo: 2; z = z_hi * 2 + z_lo), core: 2. Of those that a mesh axis runs over, the one named last changes fastest.
Arguments:
- queries: bfloat16 [2, 8192, 4096], P('seq', ('tok', 'head')), may hold values from -6 to 6
- keys: bfloat16 [2, 8192, 4096], P('seq', ('tok', 'head')), may hold values from -6 to 6
- values: bfloat16 [2, 8192, 4096], P('seq', ('tok', 'head')), may hold values from -6 to 6
- rates: float32 [2, 8, 8192], P('seq', 'head', 'tok'), may hold values from 0.00011048543 to 0.0011048544
- fast_one: float32 [8, 512, 512], P('head'), may hold values from -0.25 to 0.25
- fast_two: float32 [8, 512, 512], P('head'), may hold values from -0.25 to 0.25
- fast_three: float32 [8, 512, 512], P('head'), may hold values from -0.25 to 0.25
- grad_out: bfloat16 [2, 8192, 4096], P('seq', ('tok', 'head')), may hold values from -6 to 6
Outputs:
- grad_queries: bfloat16 [2, 8192, 4096], P('seq', ('tok', 'head'))
- grad_keys: bfloat16 [2, 8192, 4096], P('seq', ('tok', 'head'))
- grad_values: bfloat16 [2, 8192, 4096], P('seq', ('tok', 'head'))
- grad_rates: float32 [2, 8, 8192], P('seq', 'head', 'tok')
- grad_fast_one: float32 [8, 512, 512], P('head')
- grad_fast_two: float32 [8, 512, 512], P('head')
- grad_fast_three: float32 [8, 512, 512], P('head')
The draws below stay inside these ranges and needn't reach their ends.
All inputs are finite; a program needn't handle non-finite values.
Results may differ from the reference program's by a relative error of at most 0.016.
Values may be sent and summed in bfloat16 or wider, within the bound.
A program may use at most 128 MiB of HBM per device.

```python
import math
import jax
import jax.numpy as jnp
from jax import lax

P_SIZE = 512
F = 512
HEADS = 8
D = 4096
SEQS = 2
LENGTH = 8192


def block_levels(stream_key, extent, pieces, low, high):
    factor_of = 1.0
    for position, blocks in pieces:
        steps = jax.random.uniform(jax.random.fold_in(jax.random.fold_in(stream_key, 6), position), (blocks,), jnp.float32, low / len(pieces), high / len(pieces))
        factor_of = factor_of * jnp.repeat(jnp.exp(steps), extent[position] // blocks).reshape((-1,) + (1,) * (len(extent) - 1 - position))
    return factor_of


def scatter_about(key, extent, deviation, limit, cuts=(), kind=jnp.bfloat16):
    array = deviation * jax.random.normal(key, extent, jnp.float32)
    if cuts:
        array = array * block_levels(key, extent, cuts, -0.22, 0.18)
    return jnp.clip(array, -limit, limit).astype(kind)


def setup_inputs(seed: int = 0) -> dict:
    arg_keys = jax.random.split(jax.random.key(seed), 9)
    return {
        "queries": scatter_about(arg_keys[0], (SEQS, LENGTH, D), 1.0, 6.0, ((0, 2), (1, 64))),
        "keys": scatter_about(arg_keys[1], (SEQS, LENGTH, D), 1.0, 6.0, ((0, 2), (1, 64))),
        "values": scatter_about(arg_keys[2], (SEQS, LENGTH, D), 1.0, 6.0, ((0, 2), (1, 64))),
        "rates": jnp.clip(jnp.exp(math.log(0.0011048544) - 2.3025852 * jax.random.uniform(arg_keys[3], (SEQS, HEADS, LENGTH), jnp.float32) ** block_levels(arg_keys[3], (SEQS, HEADS, LENGTH), ((0, 2), (1, 8), (2, 8)), -0.2, 0.2)), 0.00011048543, 0.0011048544),
        "fast_one": scatter_about(arg_keys[4], (HEADS, P_SIZE, F), P_SIZE ** -0.5, 0.25, ((0, 8),), jnp.float32),
        "fast_two": scatter_about(arg_keys[5], (HEADS, F, P_SIZE), F ** -0.5, 0.25, ((0, 8),), jnp.float32),
        "fast_three": scatter_about(arg_keys[6], (HEADS, P_SIZE, F), P_SIZE ** -0.5, 0.25, ((0, 8),), jnp.float32),
        "grad_out": scatter_about(arg_keys[7], (SEQS, LENGTH, D), 1.0, 6.0, ((0, 2), (1, 64))),
    }


epsilon = 1e-06

def matmul(left, right):
    return jnp.dot(left.astype(jnp.bfloat16), right.astype(jnp.bfloat16), preferred_element_type=jnp.float32)

def matmul_tn(left, right):
    return lax.dot_general(left.astype(jnp.bfloat16), right.astype(jnp.bfloat16), (((0,), (0,)), ((), ())), preferred_element_type=jnp.float32)

def matmul_nt(left, right):
    return lax.dot_general(left.astype(jnp.bfloat16), right.astype(jnp.bfloat16), (((1,), (1,)), ((), ())), preferred_element_type=jnp.float32)

def activation(preact):
    squash = jax.nn.sigmoid(preact)
    swished = preact * squash
    slope_one = squash * (1.0 + preact * (1.0 - squash))
    slope_two = squash * (1.0 - squash) * (2.0 + preact * (1.0 - 2.0 * squash))
    return (squash, swished, slope_one, slope_two)

def inner_forward(keys_h, values_h, rate_h, w_one, w_two, w_three):
    pre_one = matmul(keys_h, w_one)
    pre_three = matmul(keys_h, w_three)
    parts = activation(pre_one)
    swished, slope_one = (parts[1], parts[2])
    hidden = swished * pre_three
    target = -rate_h[:, None] * values_h.astype(jnp.float32)
    grad_two = matmul_tn(hidden, target)
    back_hidden = matmul_nt(target, w_two)
    delta_one = back_hidden * pre_three * slope_one
    delta_three = back_hidden * swished
    grad_one = matmul_tn(keys_h, delta_one)
    grad_three = matmul_tn(keys_h, delta_three)
    saved = (pre_one, pre_three, target, back_hidden, delta_one, delta_three)
    return ((grad_one, grad_two, grad_three), saved)

def normalize(weight, update):
    ref_norm = jnp.sqrt(lax.optimization_barrier(jnp.sum(weight * weight, axis=-2, keepdims=True)) + epsilon)
    upd_norm = jnp.sqrt(lax.optimization_barrier(jnp.sum(update * update, axis=-2, keepdims=True)) + epsilon)
    return (update * (ref_norm / upd_norm), ref_norm, upd_norm)

def apply_backward(queries_h, cotangent, new_one, new_two, new_three):
    pre_one = matmul(queries_h, new_one)
    pre_three = matmul(queries_h, new_three)
    parts = activation(pre_one)
    swished, slope_one = (parts[1], parts[2])
    hidden = swished * pre_three
    grad_two = matmul_tn(hidden, cotangent)
    back_hidden = matmul_nt(cotangent, new_two)
    delta_one = back_hidden * pre_three * slope_one
    delta_three = back_hidden * swished
    grad_one = matmul_tn(queries_h, delta_one)
    grad_three = matmul_tn(queries_h, delta_three)
    grad_queries = matmul_nt(delta_one, new_one) + matmul_nt(delta_three, new_three)
    return ((grad_one, grad_two, grad_three), grad_queries)

def adjoint(weight, update, ref_norm, upd_norm, grad_new):
    moment = lax.optimization_barrier(jnp.sum(grad_new * update, axis=-2, keepdims=True))
    factor = ref_norm / upd_norm
    grad_update = factor * grad_new - update * (factor * moment / (upd_norm * upd_norm))
    direct = weight * (moment / (upd_norm * ref_norm)) + grad_update
    return (-grad_update, direct)

def double_backward(keys_h, values_h, rate_h, w_one, w_two, w_three, saved, cot_one, cot_two, cot_three):
    pre_one, pre_three, target, back_hidden, delta_one, delta_three = saved
    parts = activation(pre_one)
    swished, slope_one, slope_two = (parts[1], parts[2], parts[3])
    hidden = swished * pre_three
    grad_hidden = matmul_nt(target, cot_two)
    grad_target = matmul(hidden, cot_two)
    grad_delta_one = matmul(keys_h, cot_one)
    grad_delta_three = matmul(keys_h, cot_three)
    grad_keys = matmul_nt(delta_one, cot_one) + matmul_nt(delta_three, cot_three)
    grad_back = grad_delta_one * pre_three * slope_one + grad_delta_three * swished
    grad_pre_three = grad_delta_one * back_hidden * slope_one + grad_hidden * swished
    grad_pre_one = grad_delta_one * back_hidden * pre_three * slope_two + grad_delta_three * back_hidden * slope_one + grad_hidden * pre_three * slope_one
    grad_target = grad_target + matmul(grad_back, w_two)
    weight_two = matmul_tn(grad_back, target)
    grad_keys = grad_keys + (matmul_nt(grad_pre_one, w_one) + matmul_nt(grad_pre_three, w_three))
    weight_one = matmul_tn(keys_h, grad_pre_one)
    weight_three = matmul_tn(keys_h, grad_pre_three)
    grad_values = -rate_h[:, None] * grad_target
    grad_rate = -lax.optimization_barrier(jnp.sum(values_h.astype(jnp.float32) * grad_target, axis=1))
    return (grad_keys, grad_values, grad_rate, (weight_one, weight_two, weight_three))

def reference(queries, keys, values, rates, fast_one, fast_two, fast_three, grad_out):
    width = fast_one.shape[1]
    query_rows, key_rows, value_rows, rate_rows = ([], [], [], [])
    totals = [[jnp.zeros_like(fast_one[0]), jnp.zeros_like(fast_two[0]), jnp.zeros_like(fast_three[0])] for head_idx in range(HEADS)]
    for seq_idx in range(SEQS):
        query_heads, key_heads, value_heads, rate_heads = ([], [], [], [])
        for head_idx in range(HEADS):
            start = head_idx * width
            keys_h = keys[seq_idx, :, start:start + width]
            values_h = values[seq_idx, :, start:start + width]
            queries_h = queries[seq_idx, :, start:start + width]
            cotangent = grad_out[seq_idx, :, start:start + width]
            rate_h = rates[seq_idx, head_idx]
            weights = (fast_one[head_idx], fast_two[head_idx], fast_three[head_idx])
            inner, saved = inner_forward(keys_h, values_h, rate_h, weights[0], weights[1], weights[2])
            normed = [normalize(weights[index], weights[index] - inner[index]) for index in range(3)]
            grads_new, grad_queries = apply_backward(queries_h, cotangent, normed[0][0], normed[1][0], normed[2][0])
            adjoints = [adjoint(weights[index], weights[index] - inner[index], normed[index][1], normed[index][2], grads_new[index]) for index in range(3)]
            grad_keys, grad_values, grad_rate, extra = double_backward(keys_h, values_h, rate_h, weights[0], weights[1], weights[2], saved, adjoints[0][0], adjoints[1][0], adjoints[2][0])
            for index in range(3):
                totals[head_idx][index] = totals[head_idx][index] + (adjoints[index][1] + extra[index])
            query_heads.append(grad_queries.astype(jnp.bfloat16))
            key_heads.append(grad_keys.astype(jnp.bfloat16))
            value_heads.append(grad_values.astype(jnp.bfloat16))
            rate_heads.append(grad_rate)
        query_rows.append(jnp.concatenate(query_heads, axis=1))
        key_rows.append(jnp.concatenate(key_heads, axis=1))
        value_rows.append(jnp.concatenate(value_heads, axis=1))
        rate_rows.append(jnp.stack(rate_heads))
    grad_fast_one = jnp.stack([totals[head_idx][0] for head_idx in range(HEADS)])
    grad_fast_two = jnp.stack([totals[head_idx][1] for head_idx in range(HEADS)])
    grad_fast_three = jnp.stack([totals[head_idx][2] for head_idx in range(HEADS)])
    return (jnp.stack(query_rows), jnp.stack(key_rows), jnp.stack(value_rows), jnp.stack(rate_rows), grad_fast_one, grad_fast_two, grad_fast_three)
```

```python
import functools

import jax
import jax.numpy as jnp
from jax import lax
from jax.experimental import pallas as pl
from jax.experimental.pallas import tpu as pltpu
from jax.sharding import PartitionSpec as P

MESH = pl.DeviceIdType.MESH
EPS = 1e-06
BF = jnp.bfloat16
F32 = jnp.float32


def mm(a, b):
    return jnp.dot(a, b, preferred_element_type=F32)


def mm_tn(a, b):
    return lax.dot_general(a, b, (((0,), (0,)), ((), ())), preferred_element_type=F32)


def mm_nt(a, b):
    return lax.dot_general(a, b, (((1,), (1,)), ((), ())), preferred_element_type=F32)


def across(r, width):
    return jnp.concatenate([r] * (width // r.shape[-1]), axis=-1)


def kernel(T, H, *refs):
    (q, k, v, rates, w1, w2, w3, e) = refs[:8]
    (gq, gk, gv, grates, gf1, gf2, gf3) = refs[8:15]
    (kx, vx, qx, ex, wf, wb, wt, rmat) = refs[15:23]
    (hid, tgt, d1b, d3b, c1, c2, c3, c4) = refs[23:31]
    (dc1b, dc3b, gacc, gqb, gkb, gvb) = refs[31:37]
    (send_a, recv_a, send_b, recv_b, full, ush, dsh, sq_send, sq_recv, outf) = refs[37:47]
    (in_send, in_recv, w_sem, a_send, a_recv, b_send, b_recv) = refs[47:54]
    (ag_send, ag_recv, fw_send, fw_recv, s_send, s_recv, o_send, o_recv, f_sem) = refs[54:63]

    X, Y = T // 2, H // 2
    TB, PD = kx.shape[1], kx.shape[2]
    SH = full.shape[3]
    CH = 2 * TB
    t, h, s = lax.axis_index("tok"), lax.axis_index("head"), lax.axis_index("seq")
    x, c = t // 2, lax.rem(t, 2)
    y, zh = h // 2, lax.rem(h, 2)

    def head_of(dy, dz):
        return lax.rem(y + dy, Y) * 2 + lax.rem(zh + dz, 2)

    def tok_of(d):
        return lax.rem(x + d, X) * 2 + c

    partner = {"tok": x * 2 + 1 - c}
    other_seq = {"seq": 1 - s}

    def order(i):
        return i + (i // 2) * (5 - 2 * i) if Y == 4 else i

    def remote(src, dst, ss, rs, dev):
        cp = pltpu.make_async_remote_copy(
            src_ref=src, dst_ref=dst, send_sem=ss, recv_sem=rs, device_id=dev, device_id_type=MESH
        )
        return cp

    def arrived(ref, sem):
        pltpu.make_async_copy(ref, ref, sem).wait()

    barrier = pltpu.get_barrier_semaphore()
    greeted = [{"head": head_of(i // 2, i % 2)} for i in range(1, H)]
    greeted += [{"tok": tok_of(d)} for d in range(1, X)]
    greeted += [partner, other_seq]
    for dev in greeted:
        pl.semaphore_signal(barrier, inc=1, device_id=dev, device_id_type=MESH)
    pl.semaphore_wait(barrier, len(greeted))

    for n, (src, dst) in enumerate(((k, kx), (v, vx), (q, qx), (e, ex))):
        for i in range(1, H):
            dy, dz = i // 2, i % 2
            back = ((Y - dy) % Y) * 2 + dz
            peer = head_of(dy, dz)
            remote(
                src.at[0, :, pl.ds(pl.multiple_of(peer * PD, PD), PD)],
                dst.at[back],
                in_send.at[n, i],
                in_recv.at[n, back],
                {"head": peer},
            ).start()
        pltpu.make_async_copy(
            src.at[0, :, pl.ds(pl.multiple_of(h * PD, PD), PD)], dst.at[0], in_recv.at[n, 0]
        ).start()
    for j, w in enumerate((w1, w2, w3)):
        pltpu.make_async_copy(w.at[0], wf.at[j], w_sem.at[j]).start()

    @pl.loop(0, 3)
    def _(j):
        arrived(wf.at[j], w_sem.at[j])
        wb[j] = wf[j].astype(BF)
        wt[j] = wf[j, :, pl.ds(pl.multiple_of(x * 2 * SH, 2 * SH), 2 * SH)].T.reshape(2, SH, PD)

    @pl.loop(0, H)
    def _(i):
        p = head_of(i // 2, lax.rem(i, 2))
        r = rates[0, :, pl.ds(pl.multiple_of(p * TB, TB), TB)]
        rmat[i] = jnp.broadcast_to(r, (TB, TB)).T

    gacc[...] = jnp.zeros_like(gacc)

    def put(ref, dy, val):
        ref[pl.ds(dy * 2, 2)] = val.reshape(2, TB, PD)

    def get(ref, dy):
        return ref[pl.ds(dy * 2, 2)].reshape(CH, PD)

    @pl.loop(0, Y)
    def _(i):
        dy = order(i)
        for dz in range(2):
            arrived(kx.at[dy * 2 + dz], in_recv.at[0, dy * 2 + dz])
        kk = get(kx, dy)
        a1 = mm(kk, wb[0])
        a3 = mm(kk, wb[2])
        sg = jax.nn.sigmoid(a1)
        om = 1.0 - sg
        swish = a1 * sg
        slope = sg * (1.0 + a1 * om)
        slope2 = sg * om * (2.0 + a1 * (om - sg))
        hb = (swish * a3).astype(BF)
        gate = a3 * slope
        put(hid, dy, hb)
        put(c1, dy, gate)
        put(c2, dy, swish)
        for dz in range(2):
            arrived(vx.at[dy * 2 + dz], in_recv.at[1, dy * 2 + dz])
        rr = across(get_r(rmat, dy, CH, TB), PD)
        tb = (-rr * get(vx, dy).astype(F32)).astype(BF)
        put(tgt, dy, tb)
        b = mm_nt(tb, wb[1])
        db1 = (b * gate).astype(BF)
        db3 = (b * swish).astype(BF)
        put(d1b, dy, db1)
        put(d3b, dy, db3)
        put(c3, dy, b * slope)
        put(c4, dy, b * (a3 * slope2))
        gacc[1] += mm_tn(tb, hb)
        gacc[0] += mm_tn(db1, kk)
        gacc[2] += mm_tn(db3, kk)

    def scatter_start(n, j):
        g = gacc.at[j].reshape(X, 2, SH, PD)
        send_a[n, j] = g[:, 1 - c].astype(BF)
        remote(send_a.at[n, j], recv_a.at[n, j], a_send.at[n, j], a_recv.at[n, j], partner).start()

    def scatter_mid(n, j):
        g = gacc.at[j].reshape(X, 2, SH, PD)
        arrived(recv_a.at[n, j], a_recv.at[n, j])
        for d in range(1, X):
            xo = lax.rem(x + d, X)
            send_b[n, j, d - 1] = (g[xo, c] + recv_a[n, j, xo].astype(F32)).astype(BF)
            remote(
                send_b.at[n, j, d - 1],
                recv_b.at[n, j, d - 1],
                b_send.at[n, j, d - 1],
                b_recv.at[n, j, d - 1],
                {"tok": tok_of(d)},
            ).start()

    def scatter_end(n, j):
        g = gacc.at[j].reshape(X, 2, SH, PD)
        total = g[x, c] + recv_a[n, j, x].astype(F32)
        for d in range(1, X):
            arrived(recv_b.at[n, j, d - 1], b_recv.at[n, j, d - 1])
            total += recv_b[n, j, d - 1].astype(F32)
        return total

    def gather_start(n, j, val):
        full[n, j, t] = val.astype(BF)
        for d in range(1, X):
            remote(
                full.at[n, j, t],
                full.at[n, j, t],
                ag_send.at[n, j, d - 1],
                ag_recv.at[n, j, d - 1],
                {"tok": tok_of(d)},
            ).start()
        remote(full.at[n, j, t], full.at[n, j, t], fw_send.at[n, j, 0], fw_recv.at[n, j, 0], partner).start()

    def gather_mid(n, j):
        for d in range(1, X):
            src = full.at[n, j, tok_of(X - d)]
            arrived(src, ag_recv.at[n, j, d - 1])
            remote(src, src, fw_send.at[n, j, d], fw_recv.at[n, j, d], partner).start()

    def gather_end(n, j):
        for d in range(X):
            src = full.at[n, j, lax.rem(x + X - d, X) * 2 + 1 - c]
            arrived(src, fw_recv.at[n, j, d])

    JS = (1, 0, 2)
    for j in JS:
        scatter_start(0, j)
    for j in JS:
        scatter_mid(0, j)
    for j in JS:
        w = wt[j, c]
        u = w - scatter_end(0, j)
        rn = jnp.sqrt(jnp.sum(w * w, axis=1, keepdims=True) + EPS)
        un = jnp.sqrt(jnp.sum(u * u, axis=1, keepdims=True) + EPS)
        ush[j] = u
        gather_start(0, j, u * (rn / un))
    for j in JS:
        gather_mid(0, j)
    gacc[...] = jnp.zeros_like(gacc)
    for j in JS:
        gather_end(0, j)

    def whole(n, j):
        return full[n, j].reshape(PD, PD)

    @pl.loop(0, Y)
    def _(i):
        dy = order(i)
        for dz in range(2):
            arrived(qx.at[dy * 2 + dz], in_recv.at[2, dy * 2 + dz])
            arrived(ex.at[dy * 2 + dz], in_recv.at[3, dy * 2 + dz])
        qq = get(qx, dy)
        ee = get(ex, dy)
        p1 = mm_nt(qq, whole(0, 0))
        p3 = mm_nt(qq, whole(0, 2))
        sg = jax.nn.sigmoid(p1)
        swish = p1 * sg
        slope = sg * (1.0 + p1 * (1.0 - sg))
        mb = (swish * p3).astype(BF)
        dm = mm(ee, whole(0, 1))
        x1 = (dm * p3 * slope).astype(BF)
        x3 = (dm * swish).astype(BF)
        put(dc1b, dy, x1)
        put(dc3b, dy, x3)
        gacc[1] += mm_tn(ee, mb)
        gacc[0] += mm_tn(x1, qq)
        gacc[2] += mm_tn(x3, qq)

    for j in JS:
        scatter_start(1, j)
    for j in JS:
        scatter_mid(1, j)

    def send_back(n, src, dst, dy):
        for dz in range(2):
            i = dy * 2 + dz
            peer = head_of(dy, dz)
            mine = dst.at[0, :, pl.ds(pl.multiple_of(h * PD, PD), PD)]
            cp = remote(src.at[i], mine, o_send.at[n, i], o_recv.at[n, lax.rem(Y - dy, Y) * 2 + dz], {"head": peer})
            if dz:
                cp.start()
            else:
                pl.when(dy != 0)(cp.start)
                pl.when(dy == 0)(pltpu.make_async_copy(src.at[i], mine, o_recv.at[n, 0]).start)

    @pl.loop(0, Y)
    def _(i):
        dy = order(i)
        g = mm(get(dc1b, dy), whole(0, 0)) + mm(get(dc3b, dy), whole(0, 2))
        put(gqb, dy, g.astype(BF))
        send_back(0, gqb, gq, dy)

    for j in JS:
        w = wt[j, c]
        u = ush[j]
        dnew = scatter_end(1, j)
        rn = jnp.sqrt(jnp.sum(w * w, axis=1, keepdims=True) + EPS)
        un = jnp.sqrt(jnp.sum(u * u, axis=1, keepdims=True) + EPS)
        moment = jnp.sum(dnew * u, axis=1, keepdims=True)
        factor = rn / un
        du = factor * dnew - u * (factor * moment / (un * un))
        dsh[j] = w * (moment / (un * rn)) + du
        gather_start(1, j, -du)
    for j in JS:
        gather_mid(1, j)
    gacc[...] = jnp.zeros_like(gacc)
    for j in JS:
        gather_end(1, j)

    @pl.loop(0, Y)
    def _(i):
        dy = order(i)
        kk = get(kx, dy)
        tb = get(tgt, dy)
        hb = get(hid, dy)
        gate, swish, bs, bc = get(c1, dy), get(c2, dy), get(c3, dy), get(c4, dy)
        dh = mm(tb, whole(1, 1))
        dd1 = mm_nt(kk, whole(1, 0))
        dd3 = mm_nt(kk, whole(1, 2))
        dbb = (dd1 * gate + dd3 * swish).astype(BF)
        da3 = (dd1 * bs + dh * swish).astype(BF)
        da1 = (dd1 * bc + dd3 * bs + dh * gate).astype(BF)
        gk_new = (mm(get(d1b, dy), whole(1, 0)) + mm(get(d3b, dy), whole(1, 2))) + (
            mm_nt(da1, wb[0]) + mm_nt(da3, wb[2])
        )
        put(gkb, dy, gk_new.astype(BF))
        send_back(1, gkb, gk, dy)
        dt = mm_nt(hb, whole(1, 1)) + mm(dbb, wb[1])
        rr = across(get_r(rmat, dy, CH, TB), PD)
        put(gvb, dy, (-rr * dt).astype(BF))
        send_back(2, gvb, gv, dy)
        prod = get(vx, dy).astype(F32) * dt
        fold = prod[:, :TB]
        for m in range(1, PD // TB):
            fold += prod[:, m * TB : (m + 1) * TB]
        for dz in range(2):
            row = -jnp.sum(fold[dz * TB : (dz + 1) * TB].T, axis=0, keepdims=True)
            grates[0, :, pl.ds(pl.multiple_of(head_of(dy, dz) * TB, TB), TB)] = row
        gacc[1] += mm_tn(tb, dbb)
        gacc[0] += mm_tn(da1, kk)
        gacc[2] += mm_tn(da3, kk)

    for j in JS:
        scatter_start(2, j)
    for j in JS:
        scatter_mid(2, j)
    for j in JS:
        sq_send[j] = (scatter_end(2, j) + dsh[j]).astype(BF)
        remote(sq_send.at[j], sq_recv.at[j], s_send.at[j], s_recv.at[j], other_seq).start()
    for j in JS:
        arrived(sq_recv.at[j], s_recv.at[j])
        gather_start(2, j, sq_send[j].astype(F32) + sq_recv[j].astype(F32))
    for j in JS:
        gather_mid(2, j)
    outs = (gf1, gf2, gf3)
    for j in JS:
        gather_end(2, j)
        for m in range(X):
            part = full[2, j, 2 * m : 2 * m + 2].reshape(2 * SH, PD).astype(F32)
            outf[j, :, m * 2 * SH : (m + 1) * 2 * SH] = part.T
        pltpu.make_async_copy(outf.at[j], outs[j].at[0], f_sem.at[j]).start()

    for n, dst in enumerate((gq, gk, gv)):
        for i in range(H):
            mine = dst.at[0, :, pl.ds(pl.multiple_of(head_of(i // 2, i % 2) * PD, PD), PD)]
            arrived(mine, o_recv.at[n, i])
    for n, src in enumerate((gqb, gkb, gvb)):
        for i in range(1, H):
            arrived(src.at[i], o_send.at[n, i])
    for n, src in enumerate((kx, vx, qx, ex)):
        for i in range(1, H):
            arrived(src.at[i], in_send.at[n, i])
    for n in range(3):
        for j in range(3):
            arrived(send_a.at[n, j], a_send.at[n, j])
            for d in range(1, X):
                arrived(send_b.at[n, j, d - 1], b_send.at[n, j, d - 1])
                arrived(full.at[n, j, 0], ag_send.at[n, j, d - 1])
            for d in range(X):
                arrived(full.at[n, j, 0], fw_send.at[n, j, d])
    for j in range(3):
        arrived(sq_send.at[j], s_send.at[j])
        arrived(outf.at[j], f_sem.at[j])


def get_r(rmat, dy, rows, width):
    return rmat[pl.ds(dy * 2, 2)].reshape(rows, width)


def solution(mesh):
    T, H = mesh.shape["tok"], mesh.shape["head"]
    assert T % 2 == 0 and H % 2 == 0 and mesh.shape["seq"] == 2

    def body(queries, keys, values, rates, fast_one, fast_two, fast_three, grad_out):
        tb, d = queries.shape[1], queries.shape[2]
        pd = fast_one.shape[1]
        n = tb * H
        X = T // 2
        sh = pd // T
        assert d == pd * H and rates.shape[2] == n

        def vm(*shape, dtype=BF):
            return pltpu.VMEM(shape, dtype)

        dma = pltpu.SemaphoreType.DMA
        tok = lambda dtype=BF: vm(H, tb, pd, dtype=dtype)
        scratch = [
            tok(), tok(), tok(), tok(),
            vm(3, pd, pd, dtype=F32), vm(3, pd, pd), vm(3, 2, sh, pd, dtype=F32), vm(H, tb, tb, dtype=F32),
            tok(), tok(), tok(), tok(), tok(F32), tok(F32), tok(F32), tok(F32),
            tok(), tok(), vm(3, pd, pd, dtype=F32), tok(), tok(), tok(),
            vm(3, 3, X, sh, pd), vm(3, 3, X, sh, pd),
            vm(3, 3, max(X - 1, 1), sh, pd), vm(3, 3, max(X - 1, 1), sh, pd),
            vm(3, 3, T, sh, pd), vm(3, sh, pd, dtype=F32), vm(3, sh, pd, dtype=F32),
            vm(3, sh, pd), vm(3, sh, pd), vm(3, pd, pd, dtype=F32),
            dma((4, H)), dma((4, H)), dma((3,)), dma((3, 3)), dma((3, 3)),
            dma((3, 3, max(X - 1, 1))), dma((3, 3, max(X - 1, 1))),
            dma((3, 3, max(X - 1, 1))), dma((3, 3, max(X - 1, 1))),
            dma((3, 3, X)), dma((3, 3, X)), dma((3,)), dma((3,)), dma((3, H)), dma((3, H)), dma((3,)),
        ]
        anyspace = pl.BlockSpec(memory_space=pl.ANY)
        vmem = pl.BlockSpec(memory_space=pltpu.VMEM)
        shape = jax.ShapeDtypeStruct
        return pl.pallas_call(
            functools.partial(kernel, T, H),
            out_shape=(
                shape(queries.shape, BF),
                shape(queries.shape, BF),
                shape(queries.shape, BF),
                shape(rates.shape, F32),
                shape(fast_one.shape, F32),
                shape(fast_one.shape, F32),
                shape(fast_one.shape, F32),
            ),
            in_specs=[anyspace, anyspace, anyspace, vmem] + [anyspace] * 4,
            out_specs=(anyspace, anyspace, anyspace, vmem, anyspace, anyspace, anyspace),
            scratch_shapes=scratch,
            compiler_params=pltpu.CompilerParams(
                collective_id=0, has_side_effects=True, vmem_limit_bytes=62 * 1024 * 1024
            ),
            name="layer",
        )(queries, keys, values, rates, fast_one, fast_two, fast_three, grad_out)

    tokens = P("seq", ("tok", "head"), None)
    row = P("seq", "head", "tok")
    weight = P("head", None, None)
    return jax.shard_map(
        body,
        mesh=mesh,
        in_specs=(tokens, tokens, tokens, row, weight, weight, weight, tokens),
        out_specs=(tokens, tokens, tokens, row, weight, weight, weight),
        check_vma=False,
    )
```

```python
import functools

import jax
import jax.numpy as jnp
from jax import lax
from jax.experimental import pallas as pl
from jax.experimental.pallas import tpu as pltpu
from jax.sharding import PartitionSpec as P

MESH = pl.DeviceIdType.MESH
EPS = 1e-06
VLIM = 56 * 1024 * 1024
NC = 4
BF = jnp.bfloat16
F32 = jnp.float32


def mm(a, b):
    return jnp.dot(a, b, preferred_element_type=F32)


def mm_tn(a, b):
    return lax.dot_general(a, b, (((0,), (0,)), ((), ())), preferred_element_type=F32)


def mm_nt(a, b):
    return lax.dot_general(a, b, (((1,), (1,)), ((), ())), preferred_element_type=F32)


def across(r, width):
    return jnp.concatenate([r] * (width // r.shape[-1]), axis=-1)


def kernel(T, H, *refs):
    (q, k, v, rates, w1, w2, w3, e) = refs[:8]
    (gq, gk, gv, grates, gf1, gf2, gf3) = refs[8:15]
    (kx, vx, qx, ex, wf, wb, wt, rmat) = refs[15:23]
    (hid, tgt, d1b, d3b, c1, c2, c3, c4) = refs[23:31]
    (dc1b, dc3b, dbb, gacc, gqb, gkb, gvb, rsum) = refs[31:39]
    (send_a, recv_a, send_1, recv_1, send_2, recv_2, full, ush, dsh, sq_send, sq_recv) = refs[39:50]
    (in_send, in_recv, w_sem, as_sem, ar_sem, s1_sem, r1_sem, s2_sem, r2_sem) = refs[50:59]
    (gs1_sem, gr1_sem, gs2_sem, gr2_sem, fs_sem, fr_sem, qs_sem, qr_sem, o_send, o_recv) = refs[59:69]

    X, Y = T // 2, H // 2
    TB, PD = kx.shape[1], kx.shape[2]
    NC = in_send.shape[1]
    CR = TB // NC
    SH = full.shape[3]
    CH = H * CR
    t, h, s = lax.axis_index("tok"), lax.axis_index("head"), lax.axis_index("seq")
    x, c = t // 2, lax.rem(t, 2)
    y, zh = h // 2, lax.rem(h, 2)

    def head_of(dy, dz):
        return lax.rem(y + dy, Y) * 2 + lax.rem(zh + dz, 2)

    na = x + 1 - 2 * lax.rem(x, 2)
    nb = lax.rem(x + 3 + 2 * lax.rem(x, 2), 4)
    opp = lax.rem(x + 2, 4)
    SIDE = ((0, na), (1, nb))

    partner = {"tok": x * 2 + 1 - c}
    other_seq = {"seq": 1 - s}

    def part(n):
        return pl.ds(pl.multiple_of(n * CR, CR), CR)

    def remote(src, dst, ss, rs, dev):
        cp = pltpu.make_async_remote_copy(
            src_ref=src, dst_ref=dst, send_sem=ss, recv_sem=rs, device_id=dev, device_id_type=MESH
        )
        return cp

    def arrived(ref, sem):
        pltpu.make_async_copy(ref, ref, sem).wait()

    barrier = pltpu.get_barrier_semaphore()
    greeted = [{"head": head_of(i // 2, i % 2)} for i in range(1, H)]
    greeted += [{"tok": na * 2 + c}, {"tok": nb * 2 + c}, partner, other_seq]
    for dev in greeted:
        pl.semaphore_signal(barrier, inc=1, device_id=dev, device_id_type=MESH)
    pl.semaphore_wait(barrier, len(greeted))

    for a in (0, 2):

        @pl.loop(0, NC)
        def _(m):
            for n in (a, a + 1):
                src, dst = ((k, kx), (v, vx), (q, qx), (e, ex))[n]
                for i in range(H):
                    dy, dz = i // 2, i % 2
                    back = ((Y - dy) % Y) * 2 + dz
                    peer = head_of(dy, dz)
                    here = src.at[0, part(m), pl.ds(pl.multiple_of(peer * PD, PD), PD)]
                    there = dst.at[back, part(m)]
                    if i:
                        remote(here, there, in_send.at[n, m], in_recv.at[n, m], {"head": peer}).start()
                    else:
                        pltpu.make_async_copy(here, there, in_recv.at[n, m]).start()

    for j, w in enumerate((w1, w2, w3)):
        pltpu.make_async_copy(w.at[0], wf.at[j], w_sem.at[j]).start()

    @pl.loop(0, 3)
    def _(j):
        arrived(wf.at[j], w_sem.at[j])
        wb[j] = wf[j].astype(BF)
        wt[j] = wf[j, :, pl.ds(pl.multiple_of(x * 2 * SH, 2 * SH), 2 * SH)].T.reshape(2, SH, PD)

    @pl.loop(0, H)
    def _(i):
        p = head_of(i // 2, lax.rem(i, 2))
        r = rates[0, :, pl.ds(pl.multiple_of(p * TB, TB), TB)]
        rmat[i] = jnp.broadcast_to(r, (TB, TB)).T

    gacc[...] = jnp.zeros_like(gacc)

    def put(ref, m, val):
        ref[:, part(m)] = val.reshape(H, CR, val.shape[-1])

    def get(ref, m):
        return ref[:, part(m)].reshape(CH, ref.shape[-1])

    @pl.loop(0, NC)
    def _(m):
        arrived(kx.at[:, part(m)], in_recv.at[0, m])
        kk = get(kx, m)
        a1 = mm(kk, wb[0])
        a3 = mm(kk, wb[2])
        sg = jax.nn.sigmoid(a1)
        om = 1.0 - sg
        swish = a1 * sg
        slope = sg * (1.0 + a1 * om)
        slope2 = sg * om * (2.0 + a1 * (om - sg))
        hb = (swish * a3).astype(BF)
        gate = a3 * slope
        put(hid, m, hb)
        put(c1, m, gate)
        put(c2, m, swish)
        arrived(vx.at[:, part(m)], in_recv.at[1, m])
        rr = across(get(rmat, m), PD)
        tb = (-rr * get(vx, m).astype(F32)).astype(BF)
        put(tgt, m, tb)
        b = mm_nt(tb, wb[1])
        db1 = (b * gate).astype(BF)
        db3 = (b * swish).astype(BF)
        put(d1b, m, db1)
        put(d3b, m, db3)
        put(c3, m, b * slope)
        put(c4, m, b * (a3 * slope2))
        gacc[1] += mm_tn(tb, hb)
        gacc[0] += mm_tn(db1, kk)
        gacc[2] += mm_tn(db3, kk)

    HF = SH // 2

    def rows(p):
        return pl.ds(p * HF, HF)

    def cores_start(n, j):
        g = gacc.at[j].reshape(X, 2, SH, PD)
        send_a[n, j] = g[:, 1 - c].astype(BF)
        remote(send_a.at[n, j], recv_a.at[n, j], as_sem.at[n, j], ar_sem.at[n, j], partner).start()

    def chip_sum(n, j, piece, p):
        g = gacc.at[j].reshape(X, 2, SH, PD)
        return g[piece, c, rows(p)] + recv_a[n, j, piece, rows(p)].astype(F32)

    def halve_start(n, j):
        arrived(recv_a.at[n, j], ar_sem.at[n, j])
        for p, near in SIDE:
            for m, piece in enumerate((near, opp)):
                send_1[n, j, p, m] = chip_sum(n, j, piece, p).astype(BF)
            remote(
                send_1.at[n, j, p], recv_1.at[n, j, p], s1_sem.at[n, j, p], r1_sem.at[n, j, p], {"tok": near * 2 + c}
            ).start()

    def halve_again(n, j):
        for p, near in ((0, nb), (1, na)):
            arrived(recv_1.at[n, j, p], r1_sem.at[n, j, p])
            send_2[n, j, p] = (chip_sum(n, j, near, p) + recv_1[n, j, p, 1].astype(F32)).astype(BF)
            remote(
                send_2.at[n, j, p], recv_2.at[n, j, p], s2_sem.at[n, j, p], r2_sem.at[n, j, p], {"tok": near * 2 + c}
            ).start()

    def scatter_end(n, j):
        parts = []
        for p in range(2):
            arrived(recv_2.at[n, j, p], r2_sem.at[n, j, p])
            parts.append(chip_sum(n, j, x, p) + recv_1[n, j, p, 0].astype(F32) + recv_2[n, j, p].astype(F32))
        return jnp.concatenate(parts, axis=0)

    def send_rows(ref, ss, rs, dev):
        remote(ref, ref, ss, rs, dev).start()

    def gather_start(n, j, val):
        full[n, j, t] = val.astype(BF)
        mine = full.at[n, j, t]
        for p, near in SIDE:
            send_rows(mine, gs1_sem.at[n, j, p], gr1_sem.at[n, j, p], {"tok": near * 2 + c})
        send_rows(mine, fs_sem.at[n, j, 0], fr_sem.at[n, j, 0], partner)

    def gather_mid(n, j):
        for p, near in SIDE:
            got = full.at[n, j, near * 2 + c]
            arrived(got, gr1_sem.at[n, j, p])
            q, far = 1 - p, (nb, na)[p]
            send_rows(got.at[rows(q)], gs2_sem.at[n, j, q], gr2_sem.at[n, j, q], {"tok": far * 2 + c})
            send_rows(got, fs_sem.at[n, j, 1 + p], fr_sem.at[n, j, 1 + p], partner)

    def gather_far(n, j):
        for p in range(2):
            got = full.at[n, j, opp * 2 + c, rows(p)]
            arrived(got, gr2_sem.at[n, j, p])
            send_rows(got, fs_sem.at[n, j, 3 + p], fr_sem.at[n, j, 3 + p], partner)

    def gather_end(n, j):
        for m, piece in enumerate((x, na, nb)):
            arrived(full.at[n, j, piece * 2 + 1 - c], fr_sem.at[n, j, m])
        for p in range(2):
            arrived(full.at[n, j, opp * 2 + 1 - c, rows(p)], fr_sem.at[n, j, 3 + p])

    JS = (1, 0, 2)

    def each(step, n):
        for j in JS:
            step(n, j)

    each(cores_start, 0)
    each(halve_start, 0)
    each(halve_again, 0)
    for j in JS:
        w = wt[j, c]
        u = w - scatter_end(0, j)
        rn = jnp.sqrt(jnp.sum(w * w, axis=1, keepdims=True) + EPS)
        un = jnp.sqrt(jnp.sum(u * u, axis=1, keepdims=True) + EPS)
        ush[j] = u
        gather_start(0, j, u * (rn / un))
    gacc[...] = jnp.zeros_like(gacc)
    each(gather_mid, 0)
    each(gather_far, 0)
    each(gather_end, 0)

    def whole(n, j):
        return full[n, j].reshape(PD, PD)

    @pl.loop(0, NC)
    def _(m):
        arrived(qx.at[:, part(m)], in_recv.at[2, m])
        arrived(ex.at[:, part(m)], in_recv.at[3, m])
        qq = get(qx, m)
        ee = get(ex, m)
        p1 = mm_nt(qq, whole(0, 0))
        p3 = mm_nt(qq, whole(0, 2))
        sg = jax.nn.sigmoid(p1)
        swish = p1 * sg
        slope = sg * (1.0 + p1 * (1.0 - sg))
        mb = (swish * p3).astype(BF)
        dm = mm(ee, whole(0, 1))
        x1 = (dm * p3 * slope).astype(BF)
        x3 = (dm * swish).astype(BF)
        put(dc1b, m, x1)
        put(dc3b, m, x3)
        gacc[1] += mm_tn(ee, mb)
        gacc[0] += mm_tn(x1, qq)
        gacc[2] += mm_tn(x3, qq)

    each(cores_start, 1)
    each(halve_start, 1)

    def send_back(n, src, dst, m, which=(0, 1)):
        for i in range(H):
            dy, dz = i // 2, i % 2
            if dz in which:
                here = src.at[i, part(m)]
                there = dst.at[0, part(m), pl.ds(pl.multiple_of(h * PD, PD), PD)]
                if i:
                    remote(here, there, o_send.at[n, m], o_recv.at[n, m], {"head": head_of(dy, dz)}).start()
                else:
                    pltpu.make_async_copy(here, there, o_recv.at[n, m]).start()

    @pl.loop(0, NC)
    def _(m):
        g = mm(get(dc1b, m), whole(0, 0)) + mm(get(dc3b, m), whole(0, 2))
        put(gqb, m, g.astype(BF))
        send_back(0, gqb, gq, m)

    each(halve_again, 1)
    for j in JS:
        w = wt[j, c]
        u = ush[j]
        dnew = scatter_end(1, j)
        rn = jnp.sqrt(jnp.sum(w * w, axis=1, keepdims=True) + EPS)
        un = jnp.sqrt(jnp.sum(u * u, axis=1, keepdims=True) + EPS)
        moment = jnp.sum(dnew * u, axis=1, keepdims=True)
        factor = rn / un
        du = factor * dnew - u * (factor * moment / (un * un))
        dsh[j] = w * (moment / (un * rn)) + du
        gather_start(1, j, -du)
    each(gather_mid, 1)
    each(gather_far, 1)
    each(gather_end, 1)

    @pl.loop(0, NC)
    def _(m):
        kk = get(kx, m)
        tb = get(tgt, m)
        hb = get(hid, m)
        gate, swish, bs, bc = get(c1, m), get(c2, m), get(c3, m), get(c4, m)
        dh = mm(tb, whole(1, 1))
        dd1 = mm_nt(kk, whole(1, 0))
        dd3 = mm_nt(kk, whole(1, 2))
        db = (dd1 * gate + dd3 * swish).astype(BF)
        put(dbb, m, db)
        put(dc3b, m, (dd1 * bs + dh * swish).astype(BF))
        put(dc1b, m, (dd1 * bc + dd3 * bs + dh * gate).astype(BF))
        dt = mm_nt(hb, whole(1, 1)) + mm(db, wb[1])
        rr = across(get(rmat, m), PD)
        put(gvb, m, (-rr * dt).astype(BF))
        send_back(2, gvb, gv, m)
        prod = get(vx, m).astype(F32) * dt
        fold = prod[:, :TB]
        for b in range(1, PD // TB):
            fold += prod[:, b * TB : (b + 1) * TB]
        put(rsum, m, fold)

    for j, (left, right) in ((1, (tgt, dbb)), (0, (dc1b, kx)), (2, (dc3b, kx))):
        gacc[j] = mm_tn(left[...].reshape(H * TB, PD), right[...].reshape(H * TB, PD))
        cores_start(2, j)
    each(halve_start, 2)

    @pl.loop(0, NC)
    def _(m):
        g = (mm(get(d1b, m), whole(1, 0)) + mm(get(d3b, m), whole(1, 2))) + (
            mm_nt(get(dc1b, m), wb[0]) + mm_nt(get(dc3b, m), wb[2])
        )
        put(gkb, m, g.astype(BF))
        send_back(1, gkb, gk, m, (0,))

    each(halve_again, 2)
    for j in JS:
        sq_send[j] = (scatter_end(2, j) + dsh[j]).astype(BF)
        remote(sq_send.at[j], sq_recv.at[j], qs_sem.at[j], qr_sem.at[j], other_seq).start()

    @pl.loop(0, NC)
    def _(m):
        send_back(1, gkb, gk, m, (1,))

    @pl.loop(0, H)
    def _(i):
        p = head_of(i // 2, lax.rem(i, 2))
        grates[0, :, pl.ds(pl.multiple_of(p * TB, TB), TB)] = -jnp.sum(rsum[i].T, axis=0, keepdims=True)

    for j in JS:
        arrived(sq_recv.at[j], qr_sem.at[j])
        gather_start(2, j, sq_send[j].astype(F32) + sq_recv[j].astype(F32))
    each(gather_mid, 2)
    each(gather_far, 2)
    outs = (gf1, gf2, gf3)
    for j in JS:
        gather_end(2, j)
        for b in range(X):
            pair = full[2, j, 2 * b : 2 * b + 2].reshape(2 * SH, PD).astype(F32)
            outs[j][0, :, b * 2 * SH : (b + 1) * 2 * SH] = pair.T

    @pl.loop(0, NC)
    def _(m):
        for n, dst in enumerate((gq, gk, gv)):
            arrived(dst.at[0, part(m)], o_recv.at[n, m])
        for n, src in enumerate((gqb, gkb, gvb)):
            arrived(src.at[pl.ds(1, H - 1), part(m)], o_send.at[n, m])
        for n, src in enumerate((kx, vx, qx, ex)):
            arrived(src.at[pl.ds(1, H - 1), part(m)], in_send.at[n, m])

    for n in range(3):
        for j in range(3):
            arrived(send_a.at[n, j], as_sem.at[n, j])
            for p in range(2):
                arrived(send_1.at[n, j, p], s1_sem.at[n, j, p])
                arrived(send_2.at[n, j, p], s2_sem.at[n, j, p])
                arrived(full.at[n, j, 0], gs1_sem.at[n, j, p])
                arrived(full.at[n, j, 0, rows(p)], gs2_sem.at[n, j, p])
                arrived(full.at[n, j, 0, rows(p)], fs_sem.at[n, j, 3 + p])
            for m in range(3):
                arrived(full.at[n, j, 0], fs_sem.at[n, j, m])
    for j in range(3):
        arrived(sq_send.at[j], qs_sem.at[j])


def put_out(*refs):
    n = len(refs) // 2
    copies = [pltpu.make_async_copy(refs[i], refs[n + i], refs[-1].at[i]) for i in range(n)]
    for cp in copies:
        cp.start()
    for cp in copies:
        cp.wait()


def solution(mesh):
    T, H = mesh.shape["tok"], mesh.shape["head"]
    assert T == 8 and H % 2 == 0 and mesh.shape["seq"] == 2

    def body(queries, keys, values, rates, fast_one, fast_two, fast_three, grad_out):
        tb, d = queries.shape[1], queries.shape[2]
        pd = fast_one.shape[1]
        n = tb * H
        X = T // 2
        sh = pd // T
        assert d == pd * H and rates.shape[2] == n

        def vm(*shape, dtype=BF):
            return pltpu.VMEM(shape, dtype)

        dma = pltpu.SemaphoreType.DMA
        tok = lambda dtype=BF: vm(H, tb, pd, dtype=dtype)
        scratch = [
            tok(), tok(), tok(), tok(),
            vm(3, pd, pd, dtype=F32), vm(3, pd, pd), vm(3, 2, sh, pd, dtype=F32), vm(H, tb, tb, dtype=F32),
            tok(), tok(), tok(), tok(), tok(F32), tok(F32), tok(F32), tok(F32),
            tok(), tok(), tok(), vm(3, pd, pd, dtype=F32), tok(), tok(), tok(), vm(H, tb, tb, dtype=F32),
            vm(3, 3, X, sh, pd), vm(3, 3, X, sh, pd),
            vm(3, 3, 2, 2, sh // 2, pd), vm(3, 3, 2, 2, sh // 2, pd),
            vm(3, 3, 2, sh // 2, pd), vm(3, 3, 2, sh // 2, pd),
            vm(3, 3, T, sh, pd), vm(3, sh, pd, dtype=F32), vm(3, sh, pd, dtype=F32),
            vm(3, sh, pd), vm(3, sh, pd),
            dma((4, NC)), dma((4, NC)), dma((3,)), dma((3, 3)), dma((3, 3)),
            dma((3, 3, 2)), dma((3, 3, 2)), dma((3, 3, 2)), dma((3, 3, 2)),
            dma((3, 3, 2)), dma((3, 3, 2)), dma((3, 3, 2)), dma((3, 3, 2)),
            dma((3, 3, 5)), dma((3, 3, 5)), dma((3,)), dma((3,)), dma((3, NC)), dma((3, NC)),
        ]
        anyspace = pl.BlockSpec(memory_space=pl.ANY)
        vmem = pl.BlockSpec(memory_space=pltpu.VMEM)
        kinds = [(queries.shape, BF)] * 3 + [(rates.shape, F32)] + [(fast_one.shape, F32)] * 3
        held = pl.pallas_call(
            functools.partial(kernel, T, H),
            out_shape=tuple(pltpu.VMEM(a, b) for a, b in kinds),
            in_specs=[anyspace, anyspace, anyspace, vmem] + [anyspace] * 4,
            out_specs=(vmem,) * 7,
            scratch_shapes=scratch,
            compiler_params=pltpu.CompilerParams(
                collective_id=0, has_side_effects=True, vmem_limit_bytes=VLIM
            ),
            name="layer",
        )(queries, keys, values, rates, fast_one, fast_two, fast_three, grad_out)
        held = [pltpu.with_memory_space_constraint(a, pltpu.VMEM) for a in held]
        return pl.pallas_call(
            put_out,
            out_shape=tuple(jax.ShapeDtypeStruct(a, b) for a, b in kinds),
            in_specs=[vmem] * 7,
            out_specs=(anyspace,) * 7,
            scratch_shapes=[dma((7,))],
            compiler_params=pltpu.CompilerParams(vmem_limit_bytes=1024 * 1024),
            name="out",
        )(*held)

    tokens = P("seq", ("tok", "head"), None)
    row = P("seq", "head", "tok")
    weight = P("head", None, None)
    return jax.shard_map(
        body,
        mesh=mesh,
        in_specs=(tokens, tokens, tokens, row, weight, weight, weight, tokens),
        out_specs=(tokens, tokens, tokens, row, weight, weight, weight),
        check_vma=False,
    )
```

```python
import functools

import jax
import jax.numpy as jnp
from jax import lax
from jax.experimental import pallas as pl
from jax.experimental.pallas import tpu as pltpu
from jax.sharding import PartitionSpec as P

MESH = pl.DeviceIdType.MESH
EPS = 1e-06
VLIM = 56 * 1024 * 1024
NC = 4
PG = 2
BF = jnp.bfloat16
F32 = jnp.float32


def mm(a, b):
    return jnp.dot(a, b, preferred_element_type=F32)


def mm_tn(a, b):
    return lax.dot_general(a, b, (((0,), (0,)), ((), ())), preferred_element_type=F32)


def mm_nt(a, b):
    return lax.dot_general(a, b, (((1,), (1,)), ((), ())), preferred_element_type=F32)


def across(r, width):
    return jnp.concatenate([r] * (width // r.shape[-1]), axis=-1)


def kernel(T, H, *refs):
    (q, k, v, rates_in, w1, w2, w3, e) = refs[:8]
    (gq, gk, gv, grates, gf1, gf2, gf3) = refs[8:15]
    (kx, vx, qx, ex, wf, wb, wt, rmat) = refs[15:23]
    rates, rate_sem = refs[-2:]
    (hid, tgt, d1b, d3b, c1, c2, c3, c4) = refs[23:31]
    (dc1b, dc3b, dbb, gacc, gqb, gkb, gvb, rsum) = refs[31:39]
    (send_a, recv_a, send_1, recv_1, send_2, recv_2, full, ush, dsh, sq_send, sq_recv) = refs[39:50]
    (in_send, in_recv, w_sem, as_sem, ar_sem, s1_sem, r1_sem, s2_sem, r2_sem) = refs[50:59]
    (gs1_sem, gr1_sem, gs2_sem, gr2_sem, fs_sem, fr_sem, qs_sem, qr_sem, o_send, o_recv) = refs[59:69]

    X, Y = T // 2, H // 2
    TB, PD = kx.shape[1], kx.shape[2]
    NC = in_send.shape[1]
    CR = TB // NC
    SH = full.shape[3]
    CH = H * CR
    t, h, s = lax.axis_index("tok"), lax.axis_index("head"), lax.axis_index("seq")
    x, c = t // 2, lax.rem(t, 2)
    y, zh = h // 2, lax.rem(h, 2)

    def head_of(dy, dz):
        return lax.rem(y + dy, Y) * 2 + lax.rem(zh + dz, 2)

    na = x + 1 - 2 * lax.rem(x, 2)
    nb = lax.rem(x + 3 + 2 * lax.rem(x, 2), 4)
    opp = lax.rem(x + 2, 4)
    SIDE = ((0, na), (1, nb))

    partner = {"tok": x * 2 + 1 - c}
    other_seq = {"seq": 1 - s}

    def part(n):
        return pl.ds(pl.multiple_of(n * CR, CR), CR)

    def remote(src, dst, ss, rs, dev):
        cp = pltpu.make_async_remote_copy(
            src_ref=src, dst_ref=dst, send_sem=ss, recv_sem=rs, device_id=dev, device_id_type=MESH
        )
        return cp

    def arrived(ref, sem):
        pltpu.make_async_copy(ref, ref, sem).wait()

    barrier = pltpu.get_barrier_semaphore()
    greeted = [{"head": head_of(i // 2, i % 2)} for i in range(1, H)]
    greeted += [{"tok": na * 2 + c}, {"tok": nb * 2 + c}, partner, other_seq]
    for dev in greeted:
        pl.semaphore_signal(barrier, inc=1, device_id=dev, device_id_type=MESH)
    pl.semaphore_wait(barrier, len(greeted))

    for a in (0, 2):

        @pl.loop(0, NC)
        def _(m):
            for n in (a, a + 1):
                src, dst = ((k, kx), (v, vx), (q, qx), (e, ex))[n]
                for i in range(H):
                    dy, dz = i // 2, i % 2
                    back = ((Y - dy) % Y) * 2 + dz
                    peer = head_of(dy, dz)
                    here = src.at[0, part(m), pl.ds(pl.multiple_of(peer * PD, PD), PD)]
                    there = dst.at[back, part(m)]
                    if i:
                        remote(here, there, in_send.at[n, m], in_recv.at[n, m], {"head": peer}).start()
                    else:
                        pltpu.make_async_copy(here, there, in_recv.at[n, m]).start()

    pltpu.make_async_copy(rates_in.at[0], rates, rate_sem).start()
    for j, w in enumerate((w1, w2, w3)):
        pltpu.make_async_copy(w.at[0], wf.at[j], w_sem.at[j]).start()

    @pl.loop(0, 3)
    def _(j):
        arrived(wf.at[j], w_sem.at[j])
        wb[j] = wf[j].astype(BF)
        wt[j] = wf[j, :, pl.ds(pl.multiple_of(x * 2 * SH, 2 * SH), 2 * SH)].T.reshape(2, SH, PD)

    arrived(rates, rate_sem)

    @pl.loop(0, H)
    def _(i):
        p = head_of(i // 2, lax.rem(i, 2))
        r = rates[:, pl.ds(pl.multiple_of(p * TB, TB), TB)]
        rmat[i] = jnp.broadcast_to(r, (TB, TB)).T

    gacc[...] = jnp.zeros_like(gacc)

    def put(ref, m, val):
        ref[:, part(m)] = val.reshape(H, CR, val.shape[-1])

    def get(ref, m):
        return ref[:, part(m)].reshape(CH, ref.shape[-1])

    @pl.loop(0, NC)
    def _(m):
        arrived(kx.at[:, part(m)], in_recv.at[0, m])
        kk = get(kx, m)
        a1 = mm(kk, wb[0])
        a3 = mm(kk, wb[2])
        sg = jax.nn.sigmoid(a1)
        om = 1.0 - sg
        swish = a1 * sg
        slope = sg * (1.0 + a1 * om)
        slope2 = sg * om * (2.0 + a1 * (om - sg))
        hb = (swish * a3).astype(BF)
        gate = a3 * slope
        put(hid, m, hb)
        put(c1, m, gate)
        put(c2, m, swish)
        arrived(vx.at[:, part(m)], in_recv.at[1, m])
        rr = across(get(rmat, m), PD)
        tb = (-rr * get(vx, m).astype(F32)).astype(BF)
        put(tgt, m, tb)
        b = mm_nt(tb, wb[1])
        db1 = (b * gate).astype(BF)
        db3 = (b * swish).astype(BF)
        put(d1b, m, db1)
        put(d3b, m, db3)
        put(c3, m, b * slope)
        put(c4, m, b * (a3 * slope2))
        gacc[1] += mm_tn(tb, hb)
        gacc[0] += mm_tn(db1, kk)
        gacc[2] += mm_tn(db3, kk)

    QR = SH // PG
    HF = QR // 2

    def at(u):
        return u // PG, (u % PG) * QR

    def rows(p):
        return pl.ds(p * HF, HF)

    def cores_start(n, u):
        j, lo = at(u)
        g = gacc.at[j].reshape(X, 2, SH, PD)
        send_a[n, u] = g[:, 1 - c, pl.ds(lo, QR)].astype(BF)
        remote(send_a.at[n, u], recv_a.at[n, u], as_sem.at[n], ar_sem.at[n, u], partner).start()

    def chip_sum(n, u, piece, p):
        j, lo = at(u)
        g = gacc.at[j].reshape(X, 2, SH, PD)
        return g[piece, c, pl.ds(lo + p * HF, HF)] + recv_a[n, u, piece, rows(p)].astype(F32)

    def halve_start(n, u):
        arrived(recv_a.at[n, u], ar_sem.at[n, u])
        for p, near in SIDE:
            for m, piece in enumerate((near, opp)):
                send_1[n, u, p, m] = chip_sum(n, u, piece, p).astype(BF)
            remote(
                send_1.at[n, u, p], recv_1.at[n, u, p], s1_sem.at[n], r1_sem.at[n, u, p], {"tok": near * 2 + c}
            ).start()

    def halve_again(n, u):
        for p, near in ((0, nb), (1, na)):
            arrived(recv_1.at[n, u, p], r1_sem.at[n, u, p])
            send_2[n, u, p] = (chip_sum(n, u, near, p) + recv_1[n, u, p, 1].astype(F32)).astype(BF)
            remote(
                send_2.at[n, u, p], recv_2.at[n, u, p], s2_sem.at[n], r2_sem.at[n, u, p], {"tok": near * 2 + c}
            ).start()

    def scatter_end(n, u):
        parts = []
        for p in range(2):
            arrived(recv_2.at[n, u, p], r2_sem.at[n, u, p])
            parts.append(chip_sum(n, u, x, p) + recv_1[n, u, p, 0].astype(F32) + recv_2[n, u, p].astype(F32))
        return jnp.concatenate(parts, axis=0)

    def send_rows(ref, ss, rs, dev):
        remote(ref, ref, ss, rs, dev).start()

    def gather_start(n, u, val):
        j, lo = at(u)
        mine = full.at[n, j, t, pl.ds(lo, QR)]
        mine[...] = val.astype(BF)
        for p, near in SIDE:
            send_rows(mine, gs1_sem.at[n], gr1_sem.at[n, u, p], {"tok": near * 2 + c})
        send_rows(mine, fs_sem.at[n], fr_sem.at[n, j], partner)

    def gather_mid(n, u):
        j, lo = at(u)
        for p, near in SIDE:
            got = full.at[n, j, near * 2 + c, pl.ds(lo, QR)]
            arrived(got, gr1_sem.at[n, u, p])
            q, far = 1 - p, (nb, na)[p]
            half = full.at[n, j, near * 2 + c, pl.ds(lo + q * HF, HF)]
            send_rows(half, gs2_sem.at[n], gr2_sem.at[n, u, q], {"tok": far * 2 + c})
            send_rows(got, fs_sem.at[n], fr_sem.at[n, j], partner)

    def gather_far(n, u):
        j, lo = at(u)
        for p in range(2):
            arrived(full.at[n, j, opp * 2 + c, pl.ds(lo + p * HF, HF)], gr2_sem.at[n, u, p])
        send_rows(full.at[n, j, opp * 2 + c, pl.ds(lo, QR)], fs_sem.at[n], fr_sem.at[n, j], partner)

    def gather_end(n, j):
        arrived(full.at[n, j, pl.ds(0, X)], fr_sem.at[n, j])

    JS = (1, 0, 2)
    US = [j * PG + b for j in JS for b in range(PG)]

    def each(step, n):
        for u in US:
            step(n, u)

    def end(n):
        for j in JS:
            gather_end(n, j)

    each(cores_start, 0)
    each(halve_start, 0)
    each(halve_again, 0)
    for z in US:
        j, lo = at(z)
        w = wt[j, c, pl.ds(lo, QR)]
        u = w - scatter_end(0, z)
        rn = jnp.sqrt(jnp.sum(w * w, axis=1, keepdims=True) + EPS)
        un = jnp.sqrt(jnp.sum(u * u, axis=1, keepdims=True) + EPS)
        ush[j, pl.ds(lo, QR)] = u
        gather_start(0, z, u * (rn / un))
    gacc[...] = jnp.zeros_like(gacc)
    each(gather_mid, 0)
    each(gather_far, 0)
    end(0)

    def whole(n, j):
        return full[n, j].reshape(PD, PD)

    @pl.loop(0, NC)
    def _(m):
        arrived(qx.at[:, part(m)], in_recv.at[2, m])
        arrived(ex.at[:, part(m)], in_recv.at[3, m])
        qq = get(qx, m)
        ee = get(ex, m)
        p1 = mm_nt(qq, whole(0, 0))
        p3 = mm_nt(qq, whole(0, 2))
        sg = jax.nn.sigmoid(p1)
        swish = p1 * sg
        slope = sg * (1.0 + p1 * (1.0 - sg))
        mb = (swish * p3).astype(BF)
        dm = mm(ee, whole(0, 1))
        x1 = (dm * p3 * slope).astype(BF)
        x3 = (dm * swish).astype(BF)
        put(dc1b, m, x1)
        put(dc3b, m, x3)
        gacc[1] += mm_tn(ee, mb)
        gacc[0] += mm_tn(x1, qq)
        gacc[2] += mm_tn(x3, qq)

    each(cores_start, 1)
    each(halve_start, 1)

    def send_back(n, src, dst, m, which=(0, 1)):
        for i in range(H):
            dy, dz = i // 2, i % 2
            if dz in which:
                here = src.at[i, part(m)]
                there = dst.at[0, part(m), pl.ds(pl.multiple_of(h * PD, PD), PD)]
                if i:
                    remote(here, there, o_send.at[n, m], o_recv.at[n, m], {"head": head_of(dy, dz)}).start()
                else:
                    pltpu.make_async_copy(here, there, o_recv.at[n, m]).start()

    @pl.loop(0, NC)
    def _(m):
        g = mm(get(dc1b, m), whole(0, 0)) + mm(get(dc3b, m), whole(0, 2))
        put(gqb, m, g.astype(BF))
        send_back(0, gqb, gq, m)

    each(halve_again, 1)
    for z in US:
        j, lo = at(z)
        w = wt[j, c, pl.ds(lo, QR)]
        u = ush[j, pl.ds(lo, QR)]
        dnew = scatter_end(1, z)
        rn = jnp.sqrt(jnp.sum(w * w, axis=1, keepdims=True) + EPS)
        un = jnp.sqrt(jnp.sum(u * u, axis=1, keepdims=True) + EPS)
        moment = jnp.sum(dnew * u, axis=1, keepdims=True)
        factor = rn / un
        du = factor * dnew - u * (factor * moment / (un * un))
        dsh[j, pl.ds(lo, QR)] = w * (moment / (un * rn)) + du
        gather_start(1, z, -du)
    each(gather_mid, 1)
    each(gather_far, 1)
    end(1)

    @pl.loop(0, NC)
    def _(m):
        kk = get(kx, m)
        tb = get(tgt, m)
        hb = get(hid, m)
        gate, swish, bs, bc = get(c1, m), get(c2, m), get(c3, m), get(c4, m)
        dh = mm(tb, whole(1, 1))
        dd1 = mm_nt(kk, whole(1, 0))
        dd3 = mm_nt(kk, whole(1, 2))
        db = (dd1 * gate + dd3 * swish).astype(BF)
        put(dbb, m, db)
        put(dc3b, m, (dd1 * bs + dh * swish).astype(BF))
        put(dc1b, m, (dd1 * bc + dd3 * bs + dh * gate).astype(BF))
        dt = mm_nt(hb, whole(1, 1)) + mm(db, wb[1])
        rr = across(get(rmat, m), PD)
        put(gvb, m, (-rr * dt).astype(BF))
        send_back(2, gvb, gv, m)
        prod = get(vx, m).astype(F32) * dt
        fold = prod[:, :TB]
        for b in range(1, PD // TB):
            fold += prod[:, b * TB : (b + 1) * TB]
        put(rsum, m, fold)

    for j, (left, right) in ((1, (tgt, dbb)), (0, (dc1b, kx)), (2, (dc3b, kx))):
        gacc[j] = mm_tn(left[...].reshape(H * TB, PD), right[...].reshape(H * TB, PD))
        for b in range(PG):
            cores_start(2, j * PG + b)
    each(halve_start, 2)

    @pl.loop(0, NC)
    def _(m):
        g = (mm(get(d1b, m), whole(1, 0)) + mm(get(d3b, m), whole(1, 2))) + (
            mm_nt(get(dc1b, m), wb[0]) + mm_nt(get(dc3b, m), wb[2])
        )
        put(gkb, m, g.astype(BF))
        send_back(1, gkb, gk, m, (0,))
        pl.when(m < 1)(lambda: send_back(1, gkb, gk, m, (1,)))

    each(halve_again, 2)
    for u in US:
        j, lo = at(u)
        mine, theirs = sq_send.at[j, pl.ds(lo, QR)], sq_recv.at[j, pl.ds(lo, QR)]
        mine[...] = (scatter_end(2, u) + dsh[j, pl.ds(lo, QR)]).astype(BF)
        remote(mine, theirs, qs_sem, qr_sem.at[u], other_seq).start()

    @pl.loop(1, NC)
    def _(m):
        send_back(1, gkb, gk, m, (1,))

    @pl.loop(0, H)
    def _(i):
        p = head_of(i // 2, lax.rem(i, 2))
        grates[0, :, pl.ds(pl.multiple_of(p * TB, TB), TB)] = -jnp.sum(rsum[i].T, axis=0, keepdims=True)

    for u in US:
        j, lo = at(u)
        mine, theirs = sq_send.at[j, pl.ds(lo, QR)], sq_recv.at[j, pl.ds(lo, QR)]
        arrived(theirs, qr_sem.at[u])
        gather_start(2, u, mine[...].astype(F32) + theirs[...].astype(F32))
    each(gather_mid, 2)
    each(gather_far, 2)
    outs = (gf1, gf2, gf3)
    for j in JS:
        gather_end(2, j)
        for b in range(X):
            pair = full[2, j, 2 * b : 2 * b + 2].reshape(2 * SH, PD).astype(F32)
            outs[j][0, :, b * 2 * SH : (b + 1) * 2 * SH] = pair.T

    @pl.loop(0, NC)
    def _(m):
        for n, dst in enumerate((gq, gk, gv)):
            arrived(dst.at[0, part(m)], o_recv.at[n, m])
        for n, src in enumerate((gqb, gkb, gvb)):
            arrived(src.at[pl.ds(1, H - 1), part(m)], o_send.at[n, m])
        for n, src in enumerate((kx, vx, qx, ex)):
            arrived(src.at[pl.ds(1, H - 1), part(m)], in_send.at[n, m])

    for n in range(3):
        arrived(send_a.at[n], as_sem.at[n])
        arrived(send_1.at[n], s1_sem.at[n])
        arrived(send_2.at[n], s2_sem.at[n])
        arrived(full.at[n, :, pl.ds(0, 2)], gs1_sem.at[n])
        arrived(full.at[n, :, 0], gs2_sem.at[n])
        arrived(full.at[n, :, pl.ds(0, X)], fs_sem.at[n])
    arrived(sq_send, qs_sem)


def put_out(*refs):
    n = len(refs) // 2
    copies = [pltpu.make_async_copy(refs[i], refs[n + i], refs[-1].at[i]) for i in range(n)]
    for cp in copies:
        cp.start()
    for cp in copies:
        cp.wait()


def solution(mesh):
    T, H = mesh.shape["tok"], mesh.shape["head"]
    assert T == 8 and H % 2 == 0 and mesh.shape["seq"] == 2

    def body(queries, keys, values, rates, fast_one, fast_two, fast_three, grad_out):
        tb, d = queries.shape[1], queries.shape[2]
        pd = fast_one.shape[1]
        n = tb * H
        X = T // 2
        sh = pd // T
        assert d == pd * H and rates.shape[2] == n

        def vm(*shape, dtype=BF):
            return pltpu.VMEM(shape, dtype)

        dma = pltpu.SemaphoreType.DMA
        tok = lambda dtype=BF: vm(H, tb, pd, dtype=dtype)
        scratch = [
            tok(), tok(), tok(), tok(),
            vm(3, pd, pd, dtype=F32), vm(3, pd, pd), vm(3, 2, sh, pd, dtype=F32), vm(H, tb, tb, dtype=F32),
            tok(), tok(), tok(), tok(), tok(F32), tok(F32), tok(F32), tok(F32),
            tok(), tok(), tok(), vm(3, pd, pd, dtype=F32), tok(), tok(), tok(), vm(H, tb, tb, dtype=F32),
            vm(3, 3 * PG, X, sh // PG, pd), vm(3, 3 * PG, X, sh // PG, pd),
            vm(3, 3 * PG, 2, 2, sh // PG // 2, pd), vm(3, 3 * PG, 2, 2, sh // PG // 2, pd),
            vm(3, 3 * PG, 2, sh // PG // 2, pd), vm(3, 3 * PG, 2, sh // PG // 2, pd),
            vm(3, 3, T, sh, pd), vm(3, sh, pd, dtype=F32), vm(3, sh, pd, dtype=F32),
            vm(3, sh, pd), vm(3, sh, pd),
            dma((4, NC)), dma((4, NC)), dma((3,)), dma((3,)), dma((3, 3 * PG)),
            dma((3,)), dma((3, 3 * PG, 2)), dma((3,)), dma((3, 3 * PG, 2)),
            dma((3,)), dma((3, 3 * PG, 2)), dma((3,)), dma((3, 3 * PG, 2)),
            dma((3,)), dma((3, 3)), dma(()), dma((3 * PG,)), dma((3, NC)), dma((3, NC)), vm(1, n, dtype=F32), dma(()),
        ]
        anyspace = pl.BlockSpec(memory_space=pl.ANY)
        vmem = pl.BlockSpec(memory_space=pltpu.VMEM)
        kinds = [(queries.shape, BF)] * 3 + [(rates.shape, F32)] + [(fast_one.shape, F32)] * 3
        held = pl.pallas_call(
            functools.partial(kernel, T, H),
            out_shape=tuple(pltpu.VMEM(a, b) for a, b in kinds),
            in_specs=[anyspace] * 8,
            out_specs=(vmem,) * 7,
            scratch_shapes=scratch,
            compiler_params=pltpu.CompilerParams(
                collective_id=0, has_side_effects=True, vmem_limit_bytes=VLIM
            ),
            name="layer",
        )(queries, keys, values, rates, fast_one, fast_two, fast_three, grad_out)
        held = [pltpu.with_memory_space_constraint(a, pltpu.VMEM) for a in held]
        return pl.pallas_call(
            put_out,
            out_shape=tuple(jax.ShapeDtypeStruct(a, b) for a, b in kinds),
            in_specs=[vmem] * 7,
            out_specs=(anyspace,) * 7,
            scratch_shapes=[dma((7,))],
            compiler_params=pltpu.CompilerParams(vmem_limit_bytes=1024 * 1024),
            name="out",
        )(*held)

    tokens = P("seq", ("tok", "head"), None)
    row = P("seq", "head", "tok")
    weight = P("head", None, None)
    return jax.shard_map(
        body,
        mesh=mesh,
        in_specs=(tokens, tokens, tokens, row, weight, weight, weight, tokens),
        out_specs=(tokens, tokens, tokens, row, weight, weight, weight),
        check_vma=False,
    )
```

```python
import functools

import jax
import jax.numpy as jnp
from jax import lax
from jax.experimental import pallas as pl
from jax.experimental.pallas import tpu as pltpu
from jax.sharding import PartitionSpec as P

MESH = pl.DeviceIdType.MESH
EPS = 1e-06
VLIM = 56 * 1024 * 1024
NC = 4
PG = 2
BF = jnp.bfloat16
F32 = jnp.float32


def mm(a, b):
    return jnp.dot(a, b, preferred_element_type=F32)


def mm_tn(a, b):
    return lax.dot_general(a, b, (((0,), (0,)), ((), ())), preferred_element_type=F32)


def mm_nt(a, b):
    return lax.dot_general(a, b, (((1,), (1,)), ((), ())), preferred_element_type=F32)


def across(r, width):
    return jnp.concatenate([r] * (width // r.shape[-1]), axis=-1)


def kernel(T, H, *refs):
    (q, k, v, rates_in, w1, w2, w3, e) = refs[:8]
    (gq, gk, gv, grates, gf1, gf2, gf3) = refs[8:15]
    (kx, vx, qx, ex, wf, wb, wt, rmat) = refs[15:23]
    rates, rate_sem = refs[-2:]
    (hid, tgt, d1b, d3b, c1, c2, c3, c4) = refs[23:31]
    (dc1b, dc3b, dbb, gacc, gqb, gkb, gvb, rsum) = refs[31:39]
    (send_a, recv_a, send_1, recv_1, send_2, recv_2, full, ush, dsh, sq_send, sq_recv) = refs[39:50]
    (in_send, in_recv, w_sem, as_sem, ar_sem, s1_sem, r1_sem, s2_sem, r2_sem) = refs[50:59]
    (gs1_sem, gr1_sem, gs2_sem, gr2_sem, fs_sem, fr_sem, qs_sem, qr_sem, o_send, o_recv) = refs[59:69]

    X, Y = T // 2, H // 2
    TB, PD = kx.shape[1], kx.shape[2]
    NC = in_send.shape[1]
    CR = TB // NC
    SH = full.shape[3]
    CH = H * CR
    t, h, s = lax.axis_index("tok"), lax.axis_index("head"), lax.axis_index("seq")
    x, c = t // 2, lax.rem(t, 2)
    y, zh = h // 2, lax.rem(h, 2)

    def head_of(dy, dz):
        return lax.rem(y + dy, Y) * 2 + lax.rem(zh + dz, 2)

    na = x + 1 - 2 * lax.rem(x, 2)
    nb = lax.rem(x + 3 + 2 * lax.rem(x, 2), 4)
    opp = lax.rem(x + 2, 4)
    SIDE = ((0, na), (1, nb))

    partner = {"tok": x * 2 + 1 - c}
    other_seq = {"seq": 1 - s}

    def part(n):
        return pl.ds(pl.multiple_of(n * CR, CR), CR)

    def remote(src, dst, ss, rs, dev):
        cp = pltpu.make_async_remote_copy(
            src_ref=src, dst_ref=dst, send_sem=ss, recv_sem=rs, device_id=dev, device_id_type=MESH
        )
        return cp

    def arrived(ref, sem):
        pltpu.make_async_copy(ref, ref, sem).wait()

    barrier = pltpu.get_barrier_semaphore()
    greeted = [{"head": head_of(i // 2, i % 2)} for i in range(1, H)]
    greeted += [{"tok": na * 2 + c}, {"tok": nb * 2 + c}, partner, other_seq]
    for dev in greeted:
        pl.semaphore_signal(barrier, inc=1, device_id=dev, device_id_type=MESH)
    pl.semaphore_wait(barrier, len(greeted))

    for a in (0, 2):

        @pl.loop(0, NC)
        def _(m):
            for n in (a, a + 1):
                src, dst = ((k, kx), (v, vx), (q, qx), (e, ex))[n]
                for i in range(H):
                    dy, dz = i // 2, i % 2
                    back = ((Y - dy) % Y) * 2 + dz
                    peer = head_of(dy, dz)
                    here = src.at[0, part(m), pl.ds(pl.multiple_of(peer * PD, PD), PD)]
                    there = dst.at[back, part(m)]
                    if i:
                        remote(here, there, in_send.at[n, m], in_recv.at[n, m], {"head": peer}).start()
                    else:
                        pltpu.make_async_copy(here, there, in_recv.at[n, m]).start()

    pltpu.make_async_copy(rates_in.at[0], rates, rate_sem).start()
    for j, w in enumerate((w1, w2, w3)):
        pltpu.make_async_copy(w.at[0], wf.at[j], w_sem.at[j]).start()

    @pl.loop(0, 3)
    def _(j):
        arrived(wf.at[j], w_sem.at[j])
        wb[j] = wf[j].astype(BF)
        wt[j] = wf[j, :, pl.ds(pl.multiple_of(x * 2 * SH, 2 * SH), 2 * SH)].T.reshape(2, SH, PD)

    arrived(rates, rate_sem)

    @pl.loop(0, H)
    def _(i):
        p = head_of(i // 2, lax.rem(i, 2))
        r = rates[:, pl.ds(pl.multiple_of(p * TB, TB), TB)]
        rmat[i] = jnp.broadcast_to(r, (TB, TB)).T

    gacc[...] = jnp.zeros_like(gacc)

    def put(ref, m, val):
        ref[:, part(m)] = val.reshape(H, CR, val.shape[-1])

    def get(ref, m):
        return ref[:, part(m)].reshape(CH, ref.shape[-1])

    @pl.loop(0, NC)
    def _(m):
        arrived(kx.at[:, part(m)], in_recv.at[0, m])
        kk = get(kx, m)
        a1 = mm(kk, wb[0])
        a3 = mm(kk, wb[2])
        sg = jax.nn.sigmoid(a1)
        om = 1.0 - sg
        swish = a1 * sg
        slope = sg * (1.0 + a1 * om)
        slope2 = sg * om * (2.0 + a1 * (om - sg))
        hb = (swish * a3).astype(BF)
        gate = a3 * slope
        put(hid, m, hb)
        put(c1, m, gate)
        put(c2, m, swish)
        arrived(vx.at[:, part(m)], in_recv.at[1, m])
        rr = across(get(rmat, m), PD)
        tb = (-rr * get(vx, m).astype(F32)).astype(BF)
        put(tgt, m, tb)
        b = mm_nt(tb, wb[1])
        db1 = (b * gate).astype(BF)
        db3 = (b * swish).astype(BF)
        put(d1b, m, db1)
        put(d3b, m, db3)
        put(c3, m, b * slope)
        put(c4, m, b * (a3 * slope2))
        gacc[1] += mm_tn(tb, hb)
        gacc[0] += mm_tn(db1, kk)
        gacc[2] += mm_tn(db3, kk)

    QR = SH // PG
    HF = QR // 2

    def at(u):
        return u // PG, (u % PG) * QR

    def rows(p):
        return pl.ds(p * HF, HF)

    def cores_start(n, u):
        j, lo = at(u)
        g = gacc.at[j].reshape(X, 2, SH, PD)
        send_a[n, u] = g[:, 1 - c, pl.ds(lo, QR)].astype(BF)
        remote(send_a.at[n, u], recv_a.at[n, u], as_sem.at[n], ar_sem.at[n, u], partner).start()

    def chip_sum(n, u, piece, p):
        j, lo = at(u)
        g = gacc.at[j].reshape(X, 2, SH, PD)
        return g[piece, c, pl.ds(lo + p * HF, HF)] + recv_a[n, u, piece, rows(p)].astype(F32)

    def halve_start(n, u):
        arrived(recv_a.at[n, u], ar_sem.at[n, u])
        for p, near in SIDE:
            for m, piece in enumerate((near, opp)):
                send_1[n, u, p, m] = chip_sum(n, u, piece, p).astype(BF)
            remote(
                send_1.at[n, u, p], recv_1.at[n, u, p], s1_sem.at[n], r1_sem.at[n, u, p], {"tok": near * 2 + c}
            ).start()

    def halve_again(n, u):
        for p, near in ((0, nb), (1, na)):
            arrived(recv_1.at[n, u, p], r1_sem.at[n, u, p])
            send_2[n, u, p] = (chip_sum(n, u, near, p) + recv_1[n, u, p, 1].astype(F32)).astype(BF)
            remote(
                send_2.at[n, u, p], recv_2.at[n, u, p], s2_sem.at[n], r2_sem.at[n, u, p], {"tok": near * 2 + c}
            ).start()

    def scatter_end(n, u):
        parts = []
        for p in range(2):
            arrived(recv_2.at[n, u, p], r2_sem.at[n, u, p])
            parts.append(chip_sum(n, u, x, p) + recv_1[n, u, p, 0].astype(F32) + recv_2[n, u, p].astype(F32))
        return jnp.concatenate(parts, axis=0)

    def send_rows(ref, ss, rs, dev):
        remote(ref, ref, ss, rs, dev).start()

    def gather_start(n, u, val):
        j, lo = at(u)
        mine = full.at[n, j, t, pl.ds(lo, QR)]
        mine[...] = val.astype(BF)
        for p, near in SIDE:
            send_rows(mine, gs1_sem.at[n], gr1_sem.at[n, u, p], {"tok": near * 2 + c})
        send_rows(mine, fs_sem.at[n], fr_sem.at[n, j], partner)

    def gather_mid(n, u):
        j, lo = at(u)
        for p, near in SIDE:
            got = full.at[n, j, near * 2 + c, pl.ds(lo, QR)]
            arrived(got, gr1_sem.at[n, u, p])
            q, far = 1 - p, (nb, na)[p]
            half = full.at[n, j, near * 2 + c, pl.ds(lo + q * HF, HF)]
            send_rows(half, gs2_sem.at[n], gr2_sem.at[n, u, q], {"tok": far * 2 + c})
            send_rows(got, fs_sem.at[n], fr_sem.at[n, j], partner)

    def gather_far(n, u):
        j, lo = at(u)
        for p in range(2):
            arrived(full.at[n, j, opp * 2 + c, pl.ds(lo + p * HF, HF)], gr2_sem.at[n, u, p])
        send_rows(full.at[n, j, opp * 2 + c, pl.ds(lo, QR)], fs_sem.at[n], fr_sem.at[n, j], partner)

    def gather_end(n, j):
        arrived(full.at[n, j, pl.ds(0, X)], fr_sem.at[n, j])

    JS = (1, 0, 2)
    US = [j * PG + b for j in JS for b in range(PG)]

    def each(step, n):
        for u in US:
            step(n, u)

    def end(n):
        for j in JS:
            gather_end(n, j)

    each(cores_start, 0)
    each(halve_start, 0)
    each(halve_again, 0)
    for z in US:
        j, lo = at(z)
        w = wt[j, c, pl.ds(lo, QR)]
        u = w - scatter_end(0, z)
        rn = jnp.sqrt(jnp.sum(w * w, axis=1, keepdims=True) + EPS)
        un = jnp.sqrt(jnp.sum(u * u, axis=1, keepdims=True) + EPS)
        ush[j, pl.ds(lo, QR)] = u
        gather_start(0, z, u * (rn / un))
    gacc[...] = jnp.zeros_like(gacc)
    each(gather_mid, 0)
    each(gather_far, 0)
    end(0)

    def whole(n, j):
        return full[n, j].reshape(PD, PD)

    @pl.loop(0, NC)
    def _(m):
        arrived(qx.at[:, part(m)], in_recv.at[2, m])
        arrived(ex.at[:, part(m)], in_recv.at[3, m])
        qq = get(qx, m)
        ee = get(ex, m)
        p1 = mm_nt(qq, whole(0, 0))
        p3 = mm_nt(qq, whole(0, 2))
        sg = jax.nn.sigmoid(p1)
        swish = p1 * sg
        slope = sg * (1.0 + p1 * (1.0 - sg))
        mb = (swish * p3).astype(BF)
        dm = mm(ee, whole(0, 1))
        x1 = (dm * p3 * slope).astype(BF)
        x3 = (dm * swish).astype(BF)
        put(dc1b, m, x1)
        put(dc3b, m, x3)
        gacc[1] += mm_tn(ee, mb)
        gacc[0] += mm_tn(x1, qq)
        gacc[2] += mm_tn(x3, qq)

    each(cores_start, 1)
    each(halve_start, 1)

    def send_back(n, src, dst, m, which=(0, 1)):
        for i in (*range(1, H, 2), *range(2, H, 2), 0):
            dy, dz = i // 2, i % 2
            if dz in which:
                here = src.at[i, part(m)]
                there = dst.at[0, part(m), pl.ds(pl.multiple_of(h * PD, PD), PD)]
                if i:
                    remote(here, there, o_send.at[n, m], o_recv.at[n, m], {"head": head_of(dy, dz)}).start()
                else:
                    pltpu.make_async_copy(here, there, o_recv.at[n, m]).start()

    @pl.loop(0, NC)
    def _(m):
        g = mm(get(dc1b, m), whole(0, 0)) + mm(get(dc3b, m), whole(0, 2))
        put(gqb, m, g.astype(BF))
        send_back(0, gqb, gq, m)

    each(halve_again, 1)
    for z in US:
        j, lo = at(z)
        w = wt[j, c, pl.ds(lo, QR)]
        u = ush[j, pl.ds(lo, QR)]
        dnew = scatter_end(1, z)
        rn = jnp.sqrt(jnp.sum(w * w, axis=1, keepdims=True) + EPS)
        un = jnp.sqrt(jnp.sum(u * u, axis=1, keepdims=True) + EPS)
        moment = jnp.sum(dnew * u, axis=1, keepdims=True)
        factor = rn / un
        du = factor * dnew - u * (factor * moment / (un * un))
        dsh[j, pl.ds(lo, QR)] = w * (moment / (un * rn)) + du
        gather_start(1, z, -du)
    each(gather_mid, 1)
    each(gather_far, 1)
    end(1)

    @pl.loop(0, NC)
    def _(m):
        kk = get(kx, m)
        tb = get(tgt, m)
        hb = get(hid, m)
        gate, swish, bs, bc = get(c1, m), get(c2, m), get(c3, m), get(c4, m)
        dh = mm(tb, whole(1, 1))
        dd1 = mm_nt(kk, whole(1, 0))
        dd3 = mm_nt(kk, whole(1, 2))
        db = (dd1 * gate + dd3 * swish).astype(BF)
        put(dbb, m, db)
        put(dc3b, m, (dd1 * bs + dh * swish).astype(BF))
        put(dc1b, m, (dd1 * bc + dd3 * bs + dh * gate).astype(BF))
        dt = mm_nt(hb, whole(1, 1)) + mm(db, wb[1])
        rr = across(get(rmat, m), PD)
        put(gvb, m, (-rr * dt).astype(BF))
        send_back(2, gvb, gv, m)
        prod = get(vx, m).astype(F32) * dt
        fold = prod[:, :TB]
        for b in range(1, PD // TB):
            fold += prod[:, b * TB : (b + 1) * TB]
        put(rsum, m, fold)

    for j, (left, right) in ((1, (tgt, dbb)), (0, (dc1b, kx)), (2, (dc3b, kx))):
        gacc[j] = mm_tn(left[...].reshape(H * TB, PD), right[...].reshape(H * TB, PD))
        for b in range(PG):
            cores_start(2, j * PG + b)
    each(halve_start, 2)

    @pl.loop(0, NC)
    def _(m):
        g = (mm(get(d1b, m), whole(1, 0)) + mm(get(d3b, m), whole(1, 2))) + (
            mm_nt(get(dc1b, m), wb[0]) + mm_nt(get(dc3b, m), wb[2])
        )
        put(gkb, m, g.astype(BF))
        send_back(1, gkb, gk, m, (0,))
        pl.when(m < 1)(lambda: send_back(1, gkb, gk, m, (1,)))

    each(halve_again, 2)
    for u in US:
        j, lo = at(u)
        mine, theirs = sq_send.at[j, pl.ds(lo, QR)], sq_recv.at[j, pl.ds(lo, QR)]
        mine[...] = (scatter_end(2, u) + dsh[j, pl.ds(lo, QR)]).astype(BF)
        remote(mine, theirs, qs_sem, qr_sem.at[u], other_seq).start()

    @pl.loop(1, NC)
    def _(m):
        send_back(1, gkb, gk, m, (1,))

    @pl.loop(0, H)
    def _(i):
        p = head_of(i // 2, lax.rem(i, 2))
        grates[0, :, pl.ds(pl.multiple_of(p * TB, TB), TB)] = -jnp.sum(rsum[i].T, axis=0, keepdims=True)

    for u in US:
        j, lo = at(u)
        mine, theirs = sq_send.at[j, pl.ds(lo, QR)], sq_recv.at[j, pl.ds(lo, QR)]
        arrived(theirs, qr_sem.at[u])
        gather_start(2, u, mine[...].astype(F32) + theirs[...].astype(F32))
    each(gather_mid, 2)
    each(gather_far, 2)
    outs = (gf1, gf2, gf3)
    for j in JS:
        gather_end(2, j)
        for b in range(X):
            pair = full[2, j, 2 * b : 2 * b + 2].reshape(2 * SH, PD).astype(F32)
            outs[j][0, :, b * 2 * SH : (b + 1) * 2 * SH] = pair.T

    @pl.loop(0, NC)
    def _(m):
        for n, dst in enumerate((gq, gk, gv)):
            arrived(dst.at[0, part(m)], o_recv.at[n, m])
        for n, src in enumerate((gqb, gkb, gvb)):
            arrived(src.at[pl.ds(1, H - 1), part(m)], o_send.at[n, m])
        for n, src in enumerate((kx, vx, qx, ex)):
            arrived(src.at[pl.ds(1, H - 1), part(m)], in_send.at[n, m])

    for n in range(3):
        arrived(send_a.at[n], as_sem.at[n])
        arrived(send_1.at[n], s1_sem.at[n])
        arrived(send_2.at[n], s2_sem.at[n])
        arrived(full.at[n, :, pl.ds(0, 2)], gs1_sem.at[n])
        arrived(full.at[n, :, 0], gs2_sem.at[n])
        arrived(full.at[n, :, pl.ds(0, X)], fs_sem.at[n])
    arrived(sq_send, qs_sem)


def put_out(*refs):
    n = len(refs) // 2
    copies = [pltpu.make_async_copy(refs[i], refs[n + i], refs[-1].at[i]) for i in range(n)]
    for cp in copies:
        cp.start()
    for cp in copies:
        cp.wait()


def solution(mesh):
    T, H = mesh.shape["tok"], mesh.shape["head"]
    assert T == 8 and H % 2 == 0 and mesh.shape["seq"] == 2

    def body(queries, keys, values, rates, fast_one, fast_two, fast_three, grad_out):
        tb, d = queries.shape[1], queries.shape[2]
        pd = fast_one.shape[1]
        n = tb * H
        X = T // 2
        sh = pd // T
        assert d == pd * H and rates.shape[2] == n

        def vm(*shape, dtype=BF):
            return pltpu.VMEM(shape, dtype)

        dma = pltpu.SemaphoreType.DMA
        tok = lambda dtype=BF: vm(H, tb, pd, dtype=dtype)
        scratch = [
            tok(), tok(), tok(), tok(),
            vm(3, pd, pd, dtype=F32), vm(3, pd, pd), vm(3, 2, sh, pd, dtype=F32), vm(H, tb, tb, dtype=F32),
            tok(), tok(), tok(), tok(), tok(F32), tok(F32), tok(F32), tok(F32),
            tok(), tok(), tok(), vm(3, pd, pd, dtype=F32), tok(), tok(), tok(), vm(H, tb, tb, dtype=F32),
            vm(3, 3 * PG, X, sh // PG, pd), vm(3, 3 * PG, X, sh // PG, pd),
            vm(3, 3 * PG, 2, 2, sh // PG // 2, pd), vm(3, 3 * PG, 2, 2, sh // PG // 2, pd),
            vm(3, 3 * PG, 2, sh // PG // 2, pd), vm(3, 3 * PG, 2, sh // PG // 2, pd),
            vm(3, 3, T, sh, pd), vm(3, sh, pd, dtype=F32), vm(3, sh, pd, dtype=F32),
            vm(3, sh, pd), vm(3, sh, pd),
            dma((4, NC)), dma((4, NC)), dma((3,)), dma((3,)), dma((3, 3 * PG)),
            dma((3,)), dma((3, 3 * PG, 2)), dma((3,)), dma((3, 3 * PG, 2)),
            dma((3,)), dma((3, 3 * PG, 2)), dma((3,)), dma((3, 3 * PG, 2)),
            dma((3,)), dma((3, 3)), dma(()), dma((3 * PG,)), dma((3, NC)), dma((3, NC)), vm(1, n, dtype=F32), dma(()),
        ]
        anyspace = pl.BlockSpec(memory_space=pl.ANY)
        vmem = pl.BlockSpec(memory_space=pltpu.VMEM)
        kinds = [(queries.shape, BF)] * 3 + [(rates.shape, F32)] + [(fast_one.shape, F32)] * 3
        held = pl.pallas_call(
            functools.partial(kernel, T, H),
            out_shape=tuple(pltpu.VMEM(a, b) for a, b in kinds),
            in_specs=[anyspace] * 8,
            out_specs=(vmem,) * 7,
            scratch_shapes=scratch,
            compiler_params=pltpu.CompilerParams(
                collective_id=0, has_side_effects=True, vmem_limit_bytes=VLIM
            ),
            name="layer",
        )(queries, keys, values, rates, fast_one, fast_two, fast_three, grad_out)
        held = [pltpu.with_memory_space_constraint(a, pltpu.VMEM) for a in held]
        return pl.pallas_call(
            put_out,
            out_shape=tuple(jax.ShapeDtypeStruct(a, b) for a, b in kinds),
            in_specs=[vmem] * 7,
            out_specs=(anyspace,) * 7,
            scratch_shapes=[dma((7,))],
            compiler_params=pltpu.CompilerParams(vmem_limit_bytes=1024 * 1024),
            name="out",
        )(*held)

    tokens = P("seq", ("tok", "head"), None)
    row = P("seq", "head", "tok")
    weight = P("head", None, None)
    return jax.shard_map(
        body,
        mesh=mesh,
        in_specs=(tokens, tokens, tokens, row, weight, weight, weight, tokens),
        out_specs=(tokens, tokens, tokens, row, weight, weight, weight),
        check_vma=False,
    )
```
